32 devices in a mesh: parts: 2 (over y), brick: 4 (over z), tile: 2 (over x), depth: 2 (over core).
Axes of the slice: x: 2, y: 2, z: 4, core: 2. Of those that a mesh axis runs over, the one named last changes fastest.
Arguments:
- soot_extinction: bfloat16 [64, 64, 512], P(('brick', 'depth'), 'parts', 'tile'), parts along dimension 1, may hold values from 0.0099487305 to 1
- scaled_warmth: bfloat16 [64, 64, 512], P(('brick', 'depth'), 'parts', 'tile'), parts along dimension 1, may hold values from 0.5 to 2
- layer_nearness_position: int32 [16], P('parts'), parts along dimension 0, may hold values from 0 to 7, each once
Outputs:
- colour: float32 [3, 64, 512], P(None, ('parts', 'brick', 'tile', 'depth')), parts along dimension 1
- opacity: float32 [64, 512], P(('parts', 'brick', 'tile', 'depth')), parts along dimension 0
The draws below stay inside these ranges and needn't reach their ends.
There are 2 independent parts, one for each index of `parts`. The reference program is written for one: setup_inputs(seed, part) draws one part's arguments, and reference() takes and returns one part's arrays. A program takes and returns all parts, laid end to end along the dimension named above; each array names one. Nothing has to cross between parts.
Inputs may be any that keep to these rules, and one draw needn't show every extreme that they name: layer_nearness_position holds each of 0 to 7 once.
All inputs are finite; a program needn't handle non-finite values.
Results may differ from the reference program's by a relative error of at most 0.0003.
Values sent between devices are 32-bit elements; how exact they have to be, the bound alone decides.
No kernel may reach another device: no remote copies, remote signals or barrier semaphores. Data moves between devices by JAX's collectives and lax.ppermute only.
A program may use at most 64 MiB of HBM per device.

```python
import math
import jax
import jax.numpy as jnp
from jax import lax

LAYER_THICKNESS = 8
NSLAB = 8
GRID_DEPTH_COUNT = 64
STRIP_HEIGHT = 32
FRAME_WIDTH = 512


def level_of(stream_key, extent, cuts, smallest, top_value):
    def one(dim, shards_of):
        steps = jax.random.uniform(jax.random.fold_in(jax.random.fold_in(stream_key, 6), dim), (shards_of,), jnp.float32, smallest / len(cuts), top_value / len(cuts))
        return jnp.repeat(jnp.exp(steps), extent[dim] // shards_of).reshape((-1,) + (1,) * (len(extent) - dim - 1))

    loudness = one(*cuts[0])
    for cut in cuts[1:]:
        loudness = loudness * one(*cut)
    return loudness


def setup_inputs(seed: int = 0, part: int = 0) -> dict:
    seeds = jax.random.split(jax.random.key(seed), 4)
    own_keys = jax.random.split(jax.random.fold_in(seeds[3], part), 4)
    soot_extinction = jnp.clip(jnp.exp(math.log(1.0) - 4.61031033 * jax.random.uniform(own_keys[0], (GRID_DEPTH_COUNT, STRIP_HEIGHT, FRAME_WIDTH), jnp.float32) ** level_of(own_keys[0], (GRID_DEPTH_COUNT, STRIP_HEIGHT, FRAME_WIDTH), ((0, 8), (2, 2)), -0.2, 0.2)), 0.0099487305, 1.0).astype(jnp.bfloat16)
    scaled_warmth = jnp.clip(0.5 + 1.5 * jax.random.uniform(own_keys[1], (GRID_DEPTH_COUNT, STRIP_HEIGHT, FRAME_WIDTH), jnp.float32) ** level_of(own_keys[1], (GRID_DEPTH_COUNT, STRIP_HEIGHT, FRAME_WIDTH), ((0, 8), (2, 2)), -0.2, 0.2), 0.5, 2.0).astype(jnp.bfloat16)
    layer_nearness_position = jax.random.permutation(own_keys[2], NSLAB).astype(jnp.int32)
    return dict(soot_extinction=soot_extinction, scaled_warmth=scaled_warmth, layer_nearness_position=layer_nearness_position)


spectral_scale = (1.0, 1.5, 2.0)


def march_through_layer(soot_extinction, scaled_warmth, voxel_width):
    rows, cols = soot_extinction.shape[1], soot_extinction.shape[2]
    spectral = jnp.array(spectral_scale, jnp.float32)[:, None, None]

    def advance(probe_location, loop_state):
        optical, transmit, radiance = loop_state
        absorb = lax.dynamic_index_in_dim(soot_extinction, probe_location, 0, keepdims=False).astype(jnp.float32)
        thermal_glow = lax.dynamic_index_in_dim(scaled_warmth, probe_location, 0, keepdims=False).astype(jnp.float32)
        deeper = optical + voxel_width * absorb
        passed = jnp.exp(-deeper)
        source = 2.0 * jnp.exp(-spectral / thermal_glow[None])
        radiance = radiance + source * (transmit - passed)[None]
        return deeper, passed, radiance

    start = (jnp.zeros((rows, cols), jnp.float32), jnp.ones((rows, cols), jnp.float32), jnp.zeros((3, rows, cols), jnp.float32))
    optical, transmit, radiance = lax.fori_loop(0, soot_extinction.shape[0], advance, start)
    return jnp.concatenate([radiance, optical[None]], axis=0)


def reference(soot_extinction, scaled_warmth, layer_nearness_position):
    voxel_width = 12.0 / (LAYER_THICKNESS * NSLAB)

    def one_slab(slab_index):
        voxel_shift = (slab_index * LAYER_THICKNESS).astype(jnp.int32)
        block_density = lax.dynamic_slice_in_dim(soot_extinction, voxel_shift, LAYER_THICKNESS, 0)
        layer_thermal_glow = lax.dynamic_slice_in_dim(scaled_warmth, voxel_shift, LAYER_THICKNESS, 0)
        return march_through_layer(block_density, layer_thermal_glow, voxel_width)

    fields = lax.map(one_slab, jnp.arange(NSLAB, dtype=jnp.int32))
    before = (layer_nearness_position[None, :] < layer_nearness_position[:, None]).astype(jnp.float32)
    depths = fields[:, 3]
    shadow = jnp.einsum("sq,qrc->src", before, depths, precision=lax.Precision.HIGHEST)
    colour = jnp.sum(fields[:, :3] * jnp.exp(-shadow)[:, None], axis=0)
    opacity = 1.0 - jnp.exp(-jnp.sum(depths, axis=0))
    return colour, opacity
```

```python
import functools

import jax
import jax.numpy as jnp
from jax import lax
from jax.experimental import pallas as pl
from jax.experimental.pallas import tpu as pltpu
from jax.sharding import PartitionSpec as P

GROUP = ("brick", "tile", "depth")
STEP_ROWS = 16


def march(step_rows, row_count, voxel_width, soot_ref, warmth_ref, out_ref):
    layers, rows, width = soot_ref.shape

    def strip(index, carry):
        top = pl.multiple_of(index * step_rows, step_rows)
        optical = jnp.zeros((step_rows, width), jnp.float32)
        transmit = jnp.ones((step_rows, width), jnp.float32)
        radiance = [jnp.zeros((step_rows, width), jnp.float32) for _ in range(3)]
        for k in range(layers):
            absorb = soot_ref[k, pl.ds(top, step_rows), :].astype(jnp.float32)
            glow = warmth_ref[k, pl.ds(top, step_rows), :].astype(jnp.float32)
            optical = optical + voxel_width * absorb
            passed = jnp.exp(-optical)
            root = jnp.exp(-0.5 / glow)
            square = root * root
            lost = square * (transmit - passed)
            transmit = passed
            radiance[0] = radiance[0] + lost
            radiance[1] = radiance[1] + lost * root
            radiance[2] = radiance[2] + lost * square
        fields = [2.0 * radiance[0], 2.0 * radiance[1], 2.0 * radiance[2], transmit]
        owners = step_rows // row_count
        for owner in range(owners):
            for c in range(4):
                out_ref[index * owners + owner, c * row_count : (c + 1) * row_count, :] = fields[c][
                    owner * row_count : (owner + 1) * row_count, :
                ]
        return carry

    steps = rows // step_rows
    lax.fori_loop(0, steps, strip, 0, unroll=steps <= 4)


def composite(bricks, tiles, cores, position_ref, pieces_ref, colour_ref, opacity_ref, slab_at):
    slabs = bricks * cores
    row_count, width = pieces_ref.shape[1] // 4, pieces_ref.shape[2]

    def place(s, carry):
        slab_at[position_ref[s]] = s
        return carry

    lax.fori_loop(0, slabs, place, 0, unroll=slabs <= 8)
    for tile in range(tiles):

        def add(p, state):
            colour, through = state
            slab = slab_at[p]
            piece = pieces_ref[((slab // cores) * tiles + tile) * cores + slab % cores]
            colour = [
                colour[c] + piece[c * row_count : (c + 1) * row_count] * through for c in range(3)
            ]
            return colour, through * piece[3 * row_count :]

        start = (
            [jnp.zeros((row_count, width), jnp.float32) for _ in range(3)],
            jnp.ones((row_count, width), jnp.float32),
        )
        colour, through = lax.fori_loop(0, slabs, add, start, unroll=slabs <= 8)
        columns = slice(tile * width, (tile + 1) * width)
        for c in range(3):
            colour_ref[c, :, columns] = colour[c]
        opacity_ref[:, columns] = 1.0 - through


def body(soot_extinction, scaled_warmth, layer_nearness_position):
    bricks, tiles, cores = (lax.axis_size(name) for name in GROUP)
    layers, rows, width = soot_extinction.shape
    slabs, owners = bricks * cores, bricks * tiles * cores
    row_count = rows // owners
    voxel_width = 12.0 / (layers * slabs)
    vmem = pl.BlockSpec(memory_space=pltpu.VMEM)
    pieces = pl.pallas_call(
        functools.partial(march, min(STEP_ROWS, rows), row_count, voxel_width),
        out_shape=jax.ShapeDtypeStruct((owners, 4 * row_count, width), jnp.float32),
        in_specs=[vmem, vmem],
        out_specs=vmem,
        name="march",
    )(soot_extinction, scaled_warmth)
    pieces = lax.all_to_all(pieces, GROUP, split_axis=0, concat_axis=0, tiled=True)
    return pl.pallas_call(
        functools.partial(composite, bricks, tiles, cores),
        out_shape=(
            jax.ShapeDtypeStruct((3, row_count, tiles * width), jnp.float32),
            jax.ShapeDtypeStruct((row_count, tiles * width), jnp.float32),
        ),
        in_specs=[pl.BlockSpec(memory_space=pltpu.SMEM), vmem],
        scratch_shapes=[pltpu.SMEM((slabs,), jnp.int32)],
        name="composite",
    )(layer_nearness_position, pieces)


def solution(mesh):
    placed = (
        P(("brick", "depth"), "parts", "tile"),
        P(("brick", "depth"), "parts", "tile"),
        P("parts"),
    )
    return jax.shard_map(
        body,
        mesh=mesh,
        in_specs=placed,
        out_specs=(
            P(None, ("parts",) + GROUP, None),
            P(("parts",) + GROUP, None),
        ),
        check_vma=False,
    )
```

```python
import functools

import jax
import jax.numpy as jnp
from jax import lax
from jax.experimental import pallas as pl
from jax.experimental.pallas import tpu as pltpu
from jax.sharding import PartitionSpec as P

GROUP = ("brick", "tile", "depth")
STEP_ROWS = 16
VMEM_BYTES = 24 << 20


def march(step_rows, row_count, voxel_width, soot_hbm, warmth_hbm, out_ref, soot_ref, warmth_ref, arrived):
    layers, rows, width = soot_ref.shape
    steps = rows // step_rows

    def loads(index):
        window = (slice(None), pl.ds(pl.multiple_of(index * step_rows, step_rows), step_rows))
        return [
            pltpu.make_async_copy(source.at[window], held.at[window], arrived.at[index, which])
            for which, (source, held) in enumerate(
                [(soot_hbm, soot_ref), (warmth_hbm, warmth_ref)]
            )
        ]

    def fetch(index, carry):
        for copy in loads(index):
            copy.start()
        return carry

    def strip(index, carry):
        for copy in loads(index):
            copy.wait()
        top = pl.multiple_of(index * step_rows, step_rows)
        optical = jnp.zeros((step_rows, width), jnp.float32)
        transmit = jnp.ones((step_rows, width), jnp.float32)
        radiance = [jnp.zeros((step_rows, width), jnp.float32) for _ in range(3)]
        for k in range(layers):
            absorb = soot_ref[k, pl.ds(top, step_rows), :].astype(jnp.float32)
            glow = warmth_ref[k, pl.ds(top, step_rows), :].astype(jnp.float32)
            optical = optical + voxel_width * absorb
            passed = jnp.exp(-optical)
            root = jnp.exp(-0.5 / glow)
            square = root * root
            lost = square * (transmit - passed)
            transmit = passed
            radiance[0] = radiance[0] + lost
            radiance[1] = radiance[1] + lost * root
            radiance[2] = radiance[2] + lost * square
        fields = [2.0 * radiance[0], 2.0 * radiance[1], 2.0 * radiance[2], transmit]
        owners = step_rows // row_count
        for owner in range(owners):
            for c in range(4):
                out_ref[index * owners + owner, c * row_count : (c + 1) * row_count, :] = fields[c][
                    owner * row_count : (owner + 1) * row_count, :
                ]
        return carry

    lax.fori_loop(0, steps, fetch, 0, unroll=steps <= 4)
    lax.fori_loop(0, steps, strip, 0, unroll=steps <= 4)


def composite(bricks, tiles, cores, position_ref, pieces_ref, colour_ref, opacity_ref, slab_at):
    slabs = bricks * cores
    row_count, width = pieces_ref.shape[1] // 4, pieces_ref.shape[2]

    def place(s, carry):
        slab_at[position_ref[s]] = s
        return carry

    lax.fori_loop(0, slabs, place, 0, unroll=slabs <= 8)
    for tile in range(tiles):

        def add(p, state):
            colour, through = state
            slab = slab_at[p]
            piece = pieces_ref[((slab // cores) * tiles + tile) * cores + slab % cores]
            colour = [
                colour[c] + piece[c * row_count : (c + 1) * row_count] * through for c in range(3)
            ]
            return colour, through * piece[3 * row_count :]

        start = (
            [jnp.zeros((row_count, width), jnp.float32) for _ in range(3)],
            jnp.ones((row_count, width), jnp.float32),
        )
        colour, through = lax.fori_loop(0, slabs, add, start, unroll=slabs <= 8)
        columns = slice(tile * width, (tile + 1) * width)
        for c in range(3):
            colour_ref[c, :, columns] = colour[c]
        opacity_ref[:, columns] = 1.0 - through


def body(soot_extinction, scaled_warmth, layer_nearness_position):
    bricks, tiles, cores = (lax.axis_size(name) for name in GROUP)
    layers, rows, width = soot_extinction.shape
    slabs, owners = bricks * cores, bricks * tiles * cores
    row_count = rows // owners
    voxel_width = 12.0 / (layers * slabs)
    hbm = pl.BlockSpec(memory_space=pltpu.HBM)
    vmem = pl.BlockSpec(memory_space=pltpu.VMEM)
    step_rows = min(STEP_ROWS, rows)
    pieces = pl.pallas_call(
        functools.partial(march, step_rows, row_count, voxel_width),
        out_shape=jax.ShapeDtypeStruct((owners, 4 * row_count, width), jnp.float32),
        in_specs=[hbm, hbm],
        out_specs=vmem,
        scratch_shapes=[
            pltpu.VMEM(soot_extinction.shape, soot_extinction.dtype),
            pltpu.VMEM(scaled_warmth.shape, scaled_warmth.dtype),
            pltpu.SemaphoreType.DMA((rows // step_rows, 2)),
        ],
        compiler_params=pltpu.CompilerParams(vmem_limit_bytes=VMEM_BYTES),
        name="march",
    )(
        pltpu.with_memory_space_constraint(soot_extinction, pltpu.HBM),
        pltpu.with_memory_space_constraint(scaled_warmth, pltpu.HBM),
    )
    pieces = lax.all_to_all(pieces, GROUP, split_axis=0, concat_axis=0, tiled=True)
    return pl.pallas_call(
        functools.partial(composite, bricks, tiles, cores),
        out_shape=(
            jax.ShapeDtypeStruct((3, row_count, tiles * width), jnp.float32),
            jax.ShapeDtypeStruct((row_count, tiles * width), jnp.float32),
        ),
        in_specs=[pl.BlockSpec(memory_space=pltpu.SMEM), vmem],
        scratch_shapes=[pltpu.SMEM((slabs,), jnp.int32)],
        compiler_params=pltpu.CompilerParams(vmem_limit_bytes=VMEM_BYTES),
        name="composite",
    )(layer_nearness_position, pieces)


def solution(mesh):
    placed = (
        P(("brick", "depth"), "parts", "tile"),
        P(("brick", "depth"), "parts", "tile"),
        P("parts"),
    )
    return jax.shard_map(
        body,
        mesh=mesh,
        in_specs=placed,
        out_specs=(
            P(None, ("parts",) + GROUP, None),
            P(("parts",) + GROUP, None),
        ),
        check_vma=False,
    )
```

```python
import functools

import jax
import jax.numpy as jnp
from jax import lax
from jax.experimental import pallas as pl
from jax.experimental.pallas import tpu as pltpu
from jax.sharding import PartitionSpec as P

GROUP = ("brick", "tile", "depth")
STEP_ROWS = 16
VMEM_BYTES = 24 << 20


def seat(sizes, member):
    place = 0
    for size, at in zip(sizes, member):
        place = place * size + (at + size - size // 2) % size
    return place


def coordinates(sizes, index):
    bricks, tiles, cores = sizes
    return index // (tiles * cores), index // cores % tiles, index % cores


def seating(sizes):
    members = range(sizes[0] * sizes[1] * sizes[2])
    return sorted(members, key=lambda index: seat(sizes, coordinates(sizes, index)))


def march(sizes, step_rows, row_count, voxel_width, soot_hbm, warmth_hbm, out_ref, soot_ref, warmth_ref, arrived):
    layers, rows, width = soot_ref.shape
    steps = rows // step_rows

    def loads(index):
        window = (slice(None), pl.ds(pl.multiple_of(index * step_rows, step_rows), step_rows))
        return [
            pltpu.make_async_copy(source.at[window], held.at[window], arrived.at[index, which])
            for which, (source, held) in enumerate(
                [(soot_hbm, soot_ref), (warmth_hbm, warmth_ref)]
            )
        ]

    def fetch(index, carry):
        for copy in loads(index):
            copy.start()
        return carry

    def strip(index, carry):
        for copy in loads(index):
            copy.wait()
        top = pl.multiple_of(index * step_rows, step_rows)
        optical = jnp.zeros((step_rows, width), jnp.float32)
        transmit = jnp.ones((step_rows, width), jnp.float32)
        radiance = [jnp.zeros((step_rows, width), jnp.float32) for _ in range(3)]
        for k in range(layers):
            absorb = soot_ref[k, pl.ds(top, step_rows), :].astype(jnp.float32)
            glow = warmth_ref[k, pl.ds(top, step_rows), :].astype(jnp.float32)
            optical = optical + voxel_width * absorb
            passed = jnp.exp(-optical)
            root = jnp.exp(-0.5 / glow)
            square = root * root
            lost = square * (transmit - passed)
            transmit = passed
            radiance[0] = radiance[0] + lost
            radiance[1] = radiance[1] + lost * root
            radiance[2] = radiance[2] + lost * square
        fields = [2.0 * radiance[0], 2.0 * radiance[1], 2.0 * radiance[2], transmit]
        owners = step_rows // row_count
        for owner in range(owners):
            place = seat(sizes, coordinates(sizes, index * owners + owner))
            for c in range(4):
                out_ref[place, c * row_count : (c + 1) * row_count, :] = fields[c][
                    owner * row_count : (owner + 1) * row_count, :
                ]
        return carry

    lax.fori_loop(0, steps, fetch, 0, unroll=steps <= 4)
    lax.fori_loop(0, steps, strip, 0, unroll=steps <= 4)


def composite(sizes, position_ref, pieces_ref, colour_ref, opacity_ref, slab_at):
    bricks, tiles, cores = sizes
    slabs = bricks * cores
    row_count, width = pieces_ref.shape[1] // 4, pieces_ref.shape[2]

    def place(s, carry):
        slab_at[position_ref[s]] = s
        return carry

    lax.fori_loop(0, slabs, place, 0, unroll=slabs <= 8)
    for tile in range(tiles):

        def add(p, state):
            colour, through = state
            slab = slab_at[p]
            piece = pieces_ref[seat(sizes, (slab // cores, tile, slab % cores))]
            colour = [
                colour[c] + piece[c * row_count : (c + 1) * row_count] * through for c in range(3)
            ]
            return colour, through * piece[3 * row_count :]

        start = (
            [jnp.zeros((row_count, width), jnp.float32) for _ in range(3)],
            jnp.ones((row_count, width), jnp.float32),
        )
        colour, through = lax.fori_loop(0, slabs, add, start, unroll=slabs <= 8)
        columns = slice(tile * width, (tile + 1) * width)
        for c in range(3):
            colour_ref[c, :, columns] = colour[c]
        opacity_ref[:, columns] = 1.0 - through


def body(soot_extinction, scaled_warmth, layer_nearness_position):
    sizes = tuple(lax.axis_size(name) for name in GROUP)
    bricks, tiles, cores = sizes
    layers, rows, width = soot_extinction.shape
    slabs, owners = bricks * cores, bricks * tiles * cores
    row_count = rows // owners
    voxel_width = 12.0 / (layers * slabs)
    hbm = pl.BlockSpec(memory_space=pltpu.HBM)
    vmem = pl.BlockSpec(memory_space=pltpu.VMEM)
    step_rows = min(STEP_ROWS, rows)
    pieces = pl.pallas_call(
        functools.partial(march, sizes, step_rows, row_count, voxel_width),
        out_shape=jax.ShapeDtypeStruct((owners, 4 * row_count, width), jnp.float32),
        in_specs=[hbm, hbm],
        out_specs=vmem,
        scratch_shapes=[
            pltpu.VMEM(soot_extinction.shape, soot_extinction.dtype),
            pltpu.VMEM(scaled_warmth.shape, scaled_warmth.dtype),
            pltpu.SemaphoreType.DMA((rows // step_rows, 2)),
        ],
        compiler_params=pltpu.CompilerParams(vmem_limit_bytes=VMEM_BYTES),
        name="march",
    )(
        pltpu.with_memory_space_constraint(soot_extinction, pltpu.HBM),
        pltpu.with_memory_space_constraint(scaled_warmth, pltpu.HBM),
    )
    pieces = lax.all_to_all(
        pieces, GROUP, 0, 0, axis_index_groups=[seating(sizes)], tiled=True
    )
    return pl.pallas_call(
        functools.partial(composite, sizes),
        out_shape=(
            jax.ShapeDtypeStruct((3, row_count, tiles * width), jnp.float32),
            jax.ShapeDtypeStruct((row_count, tiles * width), jnp.float32),
        ),
        in_specs=[pl.BlockSpec(memory_space=pltpu.SMEM), vmem],
        scratch_shapes=[pltpu.SMEM((slabs,), jnp.int32)],
        compiler_params=pltpu.CompilerParams(vmem_limit_bytes=VMEM_BYTES),
        name="composite",
    )(layer_nearness_position, pieces)


def solution(mesh):
    placed = (
        P(("brick", "depth"), "parts", "tile"),
        P(("brick", "depth"), "parts", "tile"),
        P("parts"),
    )
    return jax.shard_map(
        body,
        mesh=mesh,
        in_specs=placed,
        out_specs=(
            P(None, ("parts",) + GROUP, None),
            P(("parts",) + GROUP, None),
        ),
        check_vma=False,
    )
```

```python
import functools
import math
import random

import jax
import jax.numpy as jnp
from jax import lax
from jax.experimental import pallas as pl
from jax.experimental.pallas import tpu as pltpu
from jax.sharding import PartitionSpec as P

GROUP = ("brick", "tile", "depth")
STEP_ROWS = 8
LANES = 128
VMEM_BYTES = 24 << 20
SEED = 42
UNROLLED = 8
LOG2E = math.log2(math.e)


def seat(sizes, member):
    place = 0
    for size, at in zip(sizes, member):
        place = place * size + (at + size - size // 2) % size
    return place


def coordinates(sizes, index):
    bricks, tiles, cores = sizes
    return index // (tiles * cores), index // cores % tiles, index % cores


def seating(sizes, unrolled):
    members = range(sizes[0] * sizes[1] * sizes[2])
    plain = sorted(members, key=lambda index: seat(sizes, coordinates(sizes, index)))
    half, corner = len(plain) // 2, list(members)[: sizes[2]]
    if not unrolled or len(plain) % 2 or half <= len(corner):
        return plain
    draw = random.Random(SEED)
    far = [index for index in plain[1:half] if index not in corner]
    draw.shuffle(far)
    even = far[: half - 1 - len(corner)] + corner
    draw.shuffle(even)
    even = plain[:1] + even
    odd = [index for index in plain if index not in even]
    draw.shuffle(odd)
    return [index for pair in zip(even, odd) for index in pair]


def seat_of(sizes, order, index):
    if isinstance(index, int):
        return order.index(index)
    return seat(sizes, coordinates(sizes, index))


def repeat(count, step, carry, unrolled):
    if not unrolled:
        return lax.fori_loop(0, count, step, carry)
    for index in range(count):
        carry = step(index, carry)
    return carry


def march(
    sizes,
    order,
    unrolled,
    step_rows,
    row_count,
    voxel_width,
    soot_hbm,
    warmth_hbm,
    position_hbm,
    out_ref,
    clear_ref,
    soot_ref,
    warmth_ref,
    position_ref,
    arrived,
    placed,
):
    layers, rows, width = soot_ref.shape
    steps = rows // step_rows
    blocks = width // LANES
    slabs = position_ref.shape[0]
    positions = pltpu.make_async_copy(position_hbm, position_ref, placed)

    def aligned(index):
        top = index * step_rows
        return top if unrolled else pl.multiple_of(top, step_rows)

    def loads(index):
        window = (slice(None), pl.ds(aligned(index), step_rows))
        return [
            pltpu.make_async_copy(source.at[window], held.at[window], arrived.at[index, which])
            for which, (source, held) in enumerate(
                [(soot_hbm, soot_ref), (warmth_hbm, warmth_ref)]
            )
        ]

    def fetch(index, carry):
        for copy in loads(index):
            copy.start()
        return carry

    def strip(index, carry):
        for copy in loads(index):
            copy.wait()
        top = aligned(index)
        absorbed = jnp.zeros((step_rows, width), jnp.float32)
        transmit = jnp.ones((step_rows, width), jnp.float32)
        radiance = [jnp.zeros((step_rows, width), jnp.float32) for _ in range(3)]
        for k in range(layers):
            absorb = soot_ref[k, pl.ds(top, step_rows), :].astype(jnp.float32)
            glow = warmth_ref[k, pl.ds(top, step_rows), :].astype(jnp.float32)
            absorbed = absorbed + absorb
            passed = jnp.exp2(absorbed * (-voxel_width * LOG2E))
            root = jnp.exp2((-0.5 * LOG2E) / glow)
            square = root * root
            lost = square * (transmit - passed)
            transmit = passed
            radiance[0] = radiance[0] + lost
            radiance[1] = radiance[1] + lost * root
            radiance[2] = radiance[2] + lost * square
        fields = [2.0 * radiance[0], 2.0 * radiance[1], 2.0 * radiance[2], transmit]
        owners = step_rows // row_count
        for owner in range(owners):
            place = seat_of(sizes, order, index * owners + owner)
            for c in range(4):
                for block in range(blocks):
                    row = (c * blocks + block) * row_count
                    out_ref[place, row : row + row_count, :] = fields[c][
                        owner * row_count : (owner + 1) * row_count,
                        block * LANES : (block + 1) * LANES,
                    ]
        return carry

    def clear(slab, carry):
        clear_ref[slab] = jnp.where(ranks < position_ref[slab], 0.0, 1.0)
        return carry

    repeat(steps, fetch, 0, unrolled)
    positions.start()
    repeat(steps, strip, 0, unrolled)
    positions.wait()
    slab_of_row = lax.broadcasted_iota(jnp.int32, clear_ref.shape[1:], 0)
    ranks = jnp.zeros(clear_ref.shape[1:], jnp.int32)
    for slab in range(slabs):
        ranks = jnp.where(slab_of_row == slab, position_ref[slab], ranks)
    repeat(slabs, clear, 0, unrolled)


def composite(sizes, order, unrolled, row_count, clear_ref, pieces_ref, colour_ref, opacity_ref):
    bricks, tiles, cores = sizes
    slabs = bricks * cores
    part = pieces_ref.shape[1] // 4
    shape = (tiles * part, LANES)

    def plane(slab, c):
        return jnp.concatenate(
            [
                pieces_ref[
                    seat_of(sizes, order, (slab // cores * tiles + tile) * cores + slab % cores),
                    c * part : (c + 1) * part,
                ]
                for tile in range(tiles)
            ],
            axis=0,
        )

    def through(slab):
        def dim(other, passed):
            return passed * jnp.maximum(plane(other, 3), clear_ref[slab, pl.ds(other, 1), :])

        return repeat(slabs, dim, jnp.ones(shape, jnp.float32), unrolled)

    def add(slab, state):
        colour, whole = state
        passed = through(slab)
        colour = [colour[c] + plane(slab, c) * passed for c in range(3)]
        return colour, whole * plane(slab, 3)

    start = ([jnp.zeros(shape, jnp.float32)] * 3, jnp.ones(shape, jnp.float32))
    colour, whole = repeat(slabs, add, start, unrolled)
    opacity = 1.0 - whole
    for block in range(shape[0] // row_count):
        rows = slice(block * row_count, (block + 1) * row_count)
        columns = slice(block * LANES, (block + 1) * LANES)
        for c in range(3):
            colour_ref[c, :, columns] = colour[c][rows]
        opacity_ref[:, columns] = opacity[rows]


def body(soot_extinction, scaled_warmth, layer_nearness_position):
    sizes = tuple(lax.axis_size(name) for name in GROUP)
    bricks, tiles, cores = sizes
    layers, rows, width = soot_extinction.shape
    slabs, owners = bricks * cores, bricks * tiles * cores
    row_count = rows // owners
    voxel_width = 12.0 / (layers * slabs)
    hbm = pl.BlockSpec(memory_space=pltpu.HBM)
    vmem = pl.BlockSpec(memory_space=pltpu.VMEM)
    step_rows = min(STEP_ROWS, rows)
    unrolled = max(slabs, rows // step_rows) <= UNROLLED
    order = seating(sizes, unrolled)
    pieces, clear = pl.pallas_call(
        functools.partial(march, sizes, order, unrolled, step_rows, row_count, voxel_width),
        out_shape=(
            jax.ShapeDtypeStruct((owners, 4 * row_count * width // LANES, LANES), jnp.float32),
            jax.ShapeDtypeStruct((slabs, slabs, LANES), jnp.float32),
        ),
        in_specs=[hbm, hbm, hbm],
        out_specs=(vmem, vmem),
        scratch_shapes=[
            pltpu.VMEM(soot_extinction.shape, soot_extinction.dtype),
            pltpu.VMEM(scaled_warmth.shape, scaled_warmth.dtype),
            pltpu.SMEM((slabs,), jnp.int32),
            pltpu.SemaphoreType.DMA((rows // step_rows, 2)),
            pltpu.SemaphoreType.DMA,
        ],
        compiler_params=pltpu.CompilerParams(vmem_limit_bytes=VMEM_BYTES),
        name="march",
    )(
        pltpu.with_memory_space_constraint(soot_extinction, pltpu.HBM),
        pltpu.with_memory_space_constraint(scaled_warmth, pltpu.HBM),
        pltpu.with_memory_space_constraint(layer_nearness_position, pltpu.HBM),
    )
    pieces = lax.all_to_all(
        pieces, GROUP, 0, 0, axis_index_groups=[order], tiled=True
    )
    return pl.pallas_call(
        functools.partial(composite, sizes, order, unrolled, row_count),
        out_shape=(
            jax.ShapeDtypeStruct((3, row_count, tiles * width), jnp.float32),
            jax.ShapeDtypeStruct((row_count, tiles * width), jnp.float32),
        ),
        in_specs=[vmem, vmem],
        compiler_params=pltpu.CompilerParams(vmem_limit_bytes=VMEM_BYTES),
        name="composite",
    )(clear, pieces)


def solution(mesh):
    placed = (
        P(("brick", "depth"), "parts", "tile"),
        P(("brick", "depth"), "parts", "tile"),
        P("parts"),
    )
    return jax.shard_map(
        body,
        mesh=mesh,
        in_specs=placed,
        out_specs=(
            P(None, ("parts",) + GROUP, None),
            P(("parts",) + GROUP, None),
        ),
        check_vma=False,
    )
```
